32 devices in a mesh: cfg: 2 (over core), seq: 8 (over z, x), tile: 2 (over y).
Axes of the slice: x: 2, y: 2, z: 4, core: 2. Of those that a mesh axis runs over, the one named last changes fastest.
Arguments:
- section_input: bfloat16 [4, 128, 64, 384], P('tile', None, 'seq'), may hold values from -6 to 6
- norm_gain: float32 [384], replicated, may hold values from 0.5 to 1.5
- conv_weight: bfloat16 [384, 864], replicated, may hold values from -0.0625 to 0.0625
- conv_bias: float32 [32], replicated, may hold values from -3 to 3
- mean_weight: float32 [32, 16], replicated, may hold values from -1 to 1
- mean_bias: float32 [16], replicated, may hold values from -3 to 3
- noisy_tokens: bfloat16 [8192, 64], P(('seq', 'tile')), may hold values from -6 to 6
- mask_tokens: bfloat16 [8192, 128], P(('seq', 'tile')), may hold values from 0 to 1
- patch_weight: bfloat16 [64, 5120], replicated, may hold values from -0.75 to 0.75
- patch_bias: float32 [5120], replicated, may hold values from -3 to 3
- context_weight: bfloat16 [192, 5120], replicated, may hold values from -0.4375 to 0.4375
- context_bias: float32 [5120], replicated, may hold values from -3 to 3
- norm_shift: float32 [5120], replicated, may hold values from -3 to 3
- norm_scale: float32 [5120], replicated, may hold values from -3 to 3
Outputs:
- block_input: bfloat16 [8192, 5120], P(('seq', 'tile'))
The draws below stay inside these ranges and needn't reach their ends.
All inputs are finite; a program needn't handle non-finite values.
Results may differ from the reference program's by a relative error of at most 0.004.
Values may be sent and summed in bfloat16 or wider, within the bound.
A program may use at most 128 MiB of HBM per device.

```python
import jax
import jax.numpy as jnp
from jax import lax

D = 5120
C = 384
Z = 16
MC = 32
K = 3
H = 128
ZO = 32
F = 4
W = 64
S = 8192
N_SEQ = 8
N_TILE = 2


def block_scale(rng, shape, shards, least, top_value):
    loudness, own = 1.0, jax.random.fold_in(rng, 6)
    for axis_at, shards_of in shards:
        draws = jnp.exp(jax.random.uniform(jax.random.fold_in(own, axis_at), (shards_of,), jnp.float32, least / len(shards), top_value / len(shards)))
        loudness = loudness * jnp.repeat(draws, shape[axis_at] // shards_of).reshape([-1 if axis == axis_at else 1 for axis in range(len(shape))])
    return loudness


def noise(key, shape, scale, most, split=(), dtype=jnp.bfloat16):
    entries = scale * jax.random.normal(key, shape, jnp.float32)
    if split:
        entries = entries * block_scale(key, shape, split, -0.22, 0.18)
    return jnp.clip(entries, -most, most).astype(dtype)


def setup_inputs(seed: int = 0) -> dict:
    key_of = jax.random.split(jax.random.key(seed), 15)
    return {
        "section_input": noise(key_of[0], (F, H, W, C), 1.0, 6.0, ((0, 2), (2, 8))),
        "norm_gain": jnp.clip(jax.random.uniform(key_of[1], (C,), jnp.float32, 0.5, 1.5), 0.5, 1.5),
        "conv_weight": noise(key_of[2], (C, K * K * K * ZO), (K * K * K * C) ** -0.5, 0.0625),
        "conv_bias": noise(key_of[3], (ZO,), 0.5, 3.0, (), jnp.float32),
        "mean_weight": noise(key_of[4], (ZO, Z), ZO ** -0.5, 1.0, (), jnp.float32),
        "mean_bias": noise(key_of[5], (Z,), 0.5, 3.0, (), jnp.float32),
        "noisy_tokens": noise(key_of[6], (S, 4 * Z), 1.0, 6.0, ((0, 16),)),
        "mask_tokens": jnp.clip(1.0 * jax.random.uniform(key_of[7], (S, 4 * MC), jnp.float32) ** block_scale(key_of[7], (S, 4 * MC), ((0, 16),), -0.2, 0.2), 0.0, 1.0).astype(jnp.bfloat16),
        "patch_weight": noise(key_of[8], (4 * Z, D), (4 * Z) ** -0.5, 0.75),
        "patch_bias": noise(key_of[9], (D,), 0.5, 3.0, (), jnp.float32),
        "context_weight": noise(key_of[10], (4 * Z + 4 * MC, D), (4 * Z + 4 * MC) ** -0.5, 0.4375),
        "context_bias": noise(key_of[11], (D,), 0.5, 3.0, (), jnp.float32),
        "norm_shift": noise(key_of[12], (D,), 0.5, 3.0, (), jnp.float32),
        "norm_scale": noise(key_of[13], (D,), 0.5, 3.0, (), jnp.float32),
    }


def reference(section_input, norm_gain, conv_weight, conv_bias, mean_weight, mean_bias, noisy_tokens, mask_tokens, patch_weight, patch_bias, context_weight, context_bias, norm_shift, norm_scale):
    frames, height, columns, channels = section_input.shape
    values = section_input.astype(jnp.float32)
    energy = lax.optimization_barrier(jnp.mean(values * values, axis=-1, keepdims=True))
    activation = jax.nn.silu(values * lax.rsqrt(energy + 1e-06) * norm_gain).astype(jnp.bfloat16)
    padded = jnp.pad(activation, ((2, 0), (1, 1), (1, 1), (0, 0)))
    kernel = conv_weight.reshape(channels, K, K, K, -1)
    out_chans = kernel.shape[-1]
    convolved = jnp.zeros((frames * height * columns, out_chans), jnp.float32)
    for step_t in range(K):
        for step_h in range(K):
            for step_w in range(K):
                window = padded[step_t:step_t + frames, step_h:step_h + height, step_w:step_w + columns]
                convolved = convolved + jnp.dot(window.reshape(-1, channels), kernel[:, step_t, step_h, step_w], preferred_element_type=jnp.float32)
    convolved = convolved + conv_bias
    latent = (jnp.dot(convolved, mean_weight, precision=lax.Precision.HIGHEST) + mean_bias).astype(jnp.bfloat16)
    latent_dim = latent.shape[-1]
    latent = latent.reshape(frames, height // 2, 2, columns // 2, 2, latent_dim)
    latent_tokens = latent.transpose(0, 1, 3, 5, 2, 4).reshape(-1, 4 * latent_dim)
    blocks = N_SEQ * N_TILE
    split_at = 4 * latent_dim

    def embed_block(pieces):
        own_latent, own_noise, own_mask = pieces
        main_part = jnp.dot(own_noise, patch_weight, preferred_element_type=jnp.float32) + patch_bias
        context_part = jnp.dot(own_latent, context_weight[:split_at], preferred_element_type=jnp.float32)
        context_part = context_part + jnp.dot(own_mask, context_weight[split_at:], preferred_element_type=jnp.float32) + context_bias
        combined = main_part + context_part
        centred = combined - lax.optimization_barrier(jnp.mean(combined, axis=-1, keepdims=True))
        variance = lax.optimization_barrier(jnp.mean(centred * centred, axis=-1, keepdims=True))
        return (centred * lax.rsqrt(variance + 1e-06) * (1.0 + norm_scale) + norm_shift).astype(jnp.bfloat16)
    result = lax.map(embed_block, (latent_tokens.reshape(blocks, -1, split_at), noisy_tokens.reshape(blocks, -1, noisy_tokens.shape[-1]), mask_tokens.reshape(blocks, -1, mask_tokens.shape[-1])))
    return result.reshape(-1, result.shape[-1])
```

```python
import functools

import jax
import jax.numpy as jnp
from jax import lax
from jax.experimental import pallas as pl
from jax.experimental.pallas import tpu as pltpu
from jax.sharding import PartitionSpec as P

K = 3
MESH = pl.DeviceIdType.MESH
F32 = jnp.float32
BF16 = jnp.bfloat16


def fold_weights(conv_weight, mean_weight):
    zo, z = mean_weight.shape
    taps = K * K * K
    width = 2 * K * 4 * 4 * z
    row = lax.broadcasted_iota(jnp.int32, (taps, zo, width), 0)
    col = lax.broadcasted_iota(jnp.int32, (taps, zo, width), 2)
    a, b, e = row // (K * K), row // K % K, row % K
    group = col // z
    g, slot, b_out, frame = group % 4, group // 4 % 4, group // 16 % K, group // (16 * K)
    e_out = jnp.where(slot == 0, 1, jnp.where(slot == 1, -1, jnp.where(slot == 2, 0, 2)))
    keep = (b == b_out) & (e == e_out) & (a == frame + 2 - g)
    high = mean_weight.astype(BF16)
    low = (mean_weight - high.astype(F32)).astype(BF16)
    copier = (
        lax.broadcasted_iota(jnp.int32, (z, width), 0)
        == lax.broadcasted_iota(jnp.int32, (z, width), 1) % z
    ).astype(BF16)
    total = None
    for part in (high, low):
        wide = jnp.dot(part, copier, preferred_element_type=F32).astype(BF16)
        mat = jnp.where(keep, wide[None], jnp.zeros((), BF16)).reshape(taps * zo, width)
        term = jnp.dot(conv_weight, mat, preferred_element_type=F32)
        total = term if total is None else total + term
    return total.astype(BF16)


def head_kernel(
    sizes, x_hbm, w_ref, gain_ref, bias_ref, out_ref,
    xin, actf, acc, edge, pk, rs_send, ls_send, ca_send, rs_got, ls_got, ca_got, patch,
    in_sem, s1_sem, r1_sem, s2_sem, r2_sem,
):
    n_c, n_s, n_t, shard_rows = sizes
    c, s, t = lax.axis_index("cfg"), lax.axis_index("seq"), lax.axis_index("tile")
    frames, height, columns, channels = x_hbm.shape
    half = height // n_c
    pairs = half // 2
    z = 16
    chunks = pairs // shard_rows
    chunk_tokens = shard_rows * (columns // 2)

    def dev(ci, si, ti):
        return {"cfg": ci, "seq": si, "tile": ti}

    load = pltpu.make_async_copy(
        x_hbm.at[:, pl.ds(c * (half - 1), half + 1)],
        xin.at[:, pl.ds(1 - c, half + 1)],
        in_sem,
    )
    load.start()

    barrier = pltpu.get_barrier_semaphore()
    links = [(1, 0), (-1, 0), (0, 1), (1, 1), (-1, 1)]

    def there(ds, dt, sign):
        si, ti = s + sign * ds, t + sign * dt
        return (si >= 0) & (si < n_s) & (ti >= 0) & (ti < n_t), si, ti

    expect = jnp.int32(0)
    for ds, dt in links:
        ok, si, ti = there(ds, dt, -1)

        @pl.when(ok)
        def _():
            pl.semaphore_signal(barrier, inc=1, device_id=dev(c, si, ti), device_id_type=MESH)

        ok, _, _ = there(ds, dt, 1)
        expect = expect + ok.astype(jnp.int32)

    first = (s * n_t + t) * shard_rows
    src_t = first // (height // 2) // frames
    src_c = first % (height // 2) // pairs
    for si in range(n_s):
        mine = (src_c == c) & (src_t == t) & (s == si)

        @pl.when(jnp.logical_not(mine))
        def _():
            pl.semaphore_signal(barrier, inc=1, device_id=dev(src_c, si, src_t), device_id_type=MESH)

    own = (src_c == c) & (src_t == t)
    expect = expect + frames * chunks * n_c - own.astype(jnp.int32)

    zero_row = jnp.zeros((frames, 1, columns, channels), BF16)

    @pl.when(c == 0)
    def _():
        xin[:, 0:1] = zero_row

    @pl.when(c == n_c - 1)
    def _():
        xin[:, half + 1 : half + 2] = zero_row

    load.wait()
    gain = gain_ref[...]
    step_rows = 6 if (half + 2) % 6 == 0 else 2
    for f in range(frames):

        @pl.loop(0, (half + 2) // step_rows)
        def _(r):
            v = xin[f, pl.ds(r * step_rows, step_rows)].astype(F32)
            v = v.reshape(step_rows * columns, channels)
            energy = jnp.sum(v * v, axis=-1, keepdims=True) * (1.0 / channels)
            v = v * lax.rsqrt(energy + 1e-06) * gain
            v = v / (1.0 + jnp.exp(-v))
            at = pl.multiple_of(r * (step_rows * columns), step_rows * columns)
            actf[f, pl.ds(at, step_rows * columns), :] = v

    rows = half * columns
    for m in range(4):
        lo = m * (rows // 4)
        total = None
        for f in range(frames):
            for b in range(K):
                lhs = actf[f, lo + b * columns : lo + b * columns + rows // 4, :].astype(BF16)
                k = (f * K + b) * 256
                term = jnp.dot(lhs, w_ref[:, k : k + 256], preferred_element_type=F32)
                total = term if total is None else total + term
        acc[lo : lo + rows // 4, :] = total[:, :128]
        edge[lo : lo + rows // 4, :] = total[:, 128:]

    q = edge[...]
    w_at = lax.broadcasted_iota(jnp.int32, (rows, 128), 0) % columns
    right = jnp.where(w_at == 0, 0.0, pltpu.roll(q, 1, 0))
    left = jnp.where(w_at == columns - 1, 0.0, pltpu.roll(q, rows - 1, 0))
    acc[...] = acc[...] + right + pltpu.roll(left, 64, 1)
    rs_send[...] = edge[pl.ds(columns - 1, half, stride=columns), :].astype(BF16)
    ls_send[...] = edge[pl.ds(0, half, stride=columns), :].astype(BF16)
    quarter = rows // 4
    lane = lax.broadcasted_iota(jnp.int32, (quarter, 128), 1)
    packed = jnp.zeros((quarter, 128), F32)
    for k in range(4):
        part = pltpu.roll(acc[k * quarter : (k + 1) * quarter, :], (k * 32 + 128 - 32) % 128, 1)
        packed = jnp.where(lane // 32 == k, part, packed)
    ca_send[...] = packed.astype(BF16)

    pl.semaphore_wait(barrier, expect)

    bufs = {1: (rs_send, rs_got), -1: (ls_send, ls_got), 0: (ca_send, ca_got)}

    def link_copy(i, sign):
        ds, dt = links[i]
        ok, si, ti = there(ds, dt, sign)
        src, dst = bufs[ds]
        if ds != 0:
            dst = dst.at[dt]
        return ok, pltpu.make_async_remote_copy(
            src_ref=src, dst_ref=dst, send_sem=s1_sem.at[i], recv_sem=r1_sem.at[i],
            device_id=dev(c, si, ti), device_id_type=MESH,
        )

    for i in (2, 3, 4, 0, 1):
        ok, copy = link_copy(i, 1)

        @pl.when(ok)
        def _():
            copy.start()

    for i in (0, 1, 3, 4, 2):
        ds, dt = links[i]
        ok, copy = link_copy(i, -1)

        @pl.when(ok)
        def _():
            copy.wait_recv()
            if ds == 0:
                got = ca_got[...].astype(F32)
                for k in range(4):
                    acc[k * quarter : (k + 1) * quarter, :] += pltpu.roll(got, (128 - 32 * k) % 128, 1)
            else:
                got = bufs[ds][1][dt].astype(F32)
                turn = (128 - 32 * dt - (64 if ds < 0 else 0)) % 128
                if turn:
                    got = pltpu.roll(got, turn, 1)
                at = pl.ds(0 if ds > 0 else columns - 1, half, stride=columns)
                acc[at, :] = acc[at, :] + got

    total = acc[...] + bias_ref[...]
    by_row = total.reshape(pairs, 2, columns, 128)
    even = by_row[:, 0].reshape(pairs * columns, 128)
    odd = by_row[:, 1].reshape(pairs * columns, 128)
    lane = lax.broadcasted_iota(jnp.int32, (pairs * columns, 128), 1)
    mixed = jnp.where(
        lane < 16, even,
        jnp.where(
            lane < 32, pltpu.roll(odd, 16, 1),
            jnp.where(lane < 48, pltpu.roll(even, 16, 1), pltpu.roll(odd, 32, 1)),
        ),
    )
    pk[...] = mixed
    tokens = pairs * columns // 2
    left_half = pk[pl.ds(0, tokens, stride=2), :]
    right_half = pk[pl.ds(1, tokens, stride=2), :]
    lane = lax.broadcasted_iota(jnp.int32, (tokens, 128), 1)
    for f in range(frames):
        one = left_half if f == 0 else pltpu.roll(left_half, 128 - 32 * f, 1)
        two = pltpu.roll(right_half, (32 - 32 * f) % 128, 1) if f != 1 else right_half
        both = jnp.where(lane < 32, one, two)
        for m in range(chunks):
            patch[f * chunks + m] = both[m * chunk_tokens : (m + 1) * chunk_tokens, :64].astype(BF16)

    def patch_copy(f, m, ci):
        shard = ((t * frames + f) * (height // 2) + c * pairs) // shard_rows + m
        si, ti = shard // n_t, shard % n_t
        mine = (si == s) & (ti == t) & (c == ci)
        piece = f * chunks + m
        local = pltpu.make_async_copy(patch.at[piece], out_ref.at[s], r2_sem.at[s])
        away = pltpu.make_async_remote_copy(
            src_ref=patch.at[piece], dst_ref=out_ref.at[s],
            send_sem=s2_sem.at[piece * n_c + ci], recv_sem=r2_sem.at[s],
            device_id=dev(ci, si, ti), device_id_type=MESH,
        )
        return mine, local, away

    every = [(f, m, ci) for f in range(frames) for m in range(chunks) for ci in range(n_c)]
    for item in every:
        mine, local, away = patch_copy(*item)

        @pl.when(mine)
        def _():
            local.start()

        @pl.when(jnp.logical_not(mine))
        def _():
            away.start()

    for si in range(n_s):
        pltpu.make_async_copy(patch.at[0], out_ref.at[si], r2_sem.at[si]).wait()
    for i in range(5):
        ok, copy = link_copy(i, 1)

        @pl.when(ok)
        def _():
            copy.wait_send()

    for item in every:
        mine, _, away = patch_copy(*item)

        @pl.when(jnp.logical_not(mine))
        def _():
            away.wait_send()


def tail_kernel(noisy, mask, lat, pw, cw, pb, cb, shift, scale, out, comb):
    split = lat.shape[1]
    width = comb.shape[1]
    step = 512
    z = split // 4
    got = lax.broadcasted_iota(jnp.int32, (split, split), 0)
    want = lax.broadcasted_iota(jnp.int32, (split, split), 1)
    perm = (want == (got % z) * 4 + (got // z % 2) * 2 + got // (2 * z)).astype(BF16)
    tokens = jnp.dot(lat[...], perm, preferred_element_type=F32).astype(BF16)
    total = None
    for k in range(0, width, step):
        at = slice(k, k + step)
        part = jnp.dot(noisy[...], pw[:, at], preferred_element_type=F32)
        part = part + jnp.dot(tokens, cw[:split, at], preferred_element_type=F32)
        part = part + jnp.dot(mask[...], cw[split:, at], preferred_element_type=F32)
        part = part + (pb[:, at] + cb[:, at])
        comb[:, at] = part
        term = jnp.sum(part, axis=-1, keepdims=True)
        total = term if total is None else total + term
    mean = total * (1.0 / width)
    square = None
    for k in range(0, width, step):
        d = comb[:, k : k + step] - mean
        term = jnp.sum(d * d, axis=-1, keepdims=True)
        square = term if square is None else square + term
    inv = lax.rsqrt(square * (1.0 / width) + 1e-06)
    for k in range(0, width, step):
        at = slice(k, k + step)
        out[:, at] = ((comb[:, at] - mean) * inv * (1.0 + scale[:, at]) + shift[:, at]).astype(BF16)


def body(
    section_input, norm_gain, conv_weight, conv_bias, mean_weight, mean_bias, noisy_tokens,
    mask_tokens, patch_weight, patch_bias, context_weight, context_bias, norm_shift, norm_scale,
):
    frames, height, columns, channels = section_input.shape
    n_c, n_s, n_t = lax.axis_size("cfg"), lax.axis_size("seq"), lax.axis_size("tile")
    z = mean_weight.shape[1]
    tokens = noisy_tokens.shape[0]
    shard_rows = tokens // (n_s * columns // 2)
    half = height // n_c
    rows = half * columns
    chunks = half // 2 // shard_rows
    chunk_tokens = shard_rows * (columns // 2)
    weight = fold_weights(conv_weight, mean_weight)
    bias = jnp.dot(conv_bias[None], mean_weight, precision=lax.Precision.HIGHEST) + mean_bias
    bias = jnp.tile(bias, (1, 128 // z))
    vmem = pl.BlockSpec(memory_space=pltpu.VMEM)
    arrived = pl.pallas_call(
        functools.partial(head_kernel, (n_c, n_s, n_t, shard_rows)),
        out_shape=jax.ShapeDtypeStruct((n_s, chunk_tokens, 4 * z), BF16),
        in_specs=[pl.BlockSpec(memory_space=pl.ANY), vmem, vmem, vmem],
        out_specs=vmem,
        scratch_shapes=[
            pltpu.VMEM((frames, half + 2, columns, channels), BF16),
            pltpu.VMEM((frames, (half + 2) * columns, channels), F32),
            pltpu.VMEM((rows, 128), F32),
            pltpu.VMEM((rows, 128), F32),
            pltpu.VMEM((rows // 2, 128), F32),
            pltpu.VMEM((half, 128), BF16),
            pltpu.VMEM((half, 128), BF16),
            pltpu.VMEM((rows // 4, 128), BF16),
            pltpu.VMEM((2, half, 128), BF16),
            pltpu.VMEM((2, half, 128), BF16),
            pltpu.VMEM((rows // 4, 128), BF16),
            pltpu.VMEM((frames * chunks, chunk_tokens, 4 * z), BF16),
            pltpu.SemaphoreType.DMA,
            pltpu.SemaphoreType.DMA((5,)),
            pltpu.SemaphoreType.DMA((5,)),
            pltpu.SemaphoreType.DMA((frames * chunks * n_c,)),
            pltpu.SemaphoreType.DMA((n_s,)),
        ],
        compiler_params=pltpu.CompilerParams(collective_id=0, has_side_effects=True),
        name="head",
    )(section_input, weight, norm_gain[None], bias)
    lat = arrived.reshape(n_s, shard_rows, columns // 2, 4 * z).transpose(1, 0, 2, 3)
    lat = lat.reshape(tokens, 4 * z)

    width = patch_weight.shape[1]
    block = min(tokens, 128)
    tok = lambda n: pl.BlockSpec((block, n), lambda i: (i, 0))
    full = lambda a: pl.BlockSpec(a.shape, lambda i: (0, 0))
    vecs = [v[None] for v in (patch_bias, context_bias, norm_shift, norm_scale)]
    return pl.pallas_call(
        tail_kernel,
        out_shape=jax.ShapeDtypeStruct((tokens, width), BF16),
        grid=(tokens // block,),
        in_specs=[tok(noisy_tokens.shape[1]), tok(mask_tokens.shape[1]), tok(4 * z)]
        + [full(a) for a in (patch_weight, context_weight)]
        + [full(v) for v in vecs],
        out_specs=tok(width),
        scratch_shapes=[pltpu.VMEM((block, width), F32)],
        name="tail",
    )(noisy_tokens, mask_tokens, lat, patch_weight, context_weight, *vecs)


def solution(mesh):
    placed = (P("tile", None, "seq", None),) + (P(),) * 5
    placed = placed + (P(("seq", "tile"), None),) * 2 + (P(),) * 6
    return jax.shard_map(
        body, mesh=mesh, in_specs=placed, out_specs=P(("seq", "tile"), None), check_vma=False
    )
```

```python
import functools

import jax
import jax.numpy as jnp
from jax import lax
from jax.experimental import pallas as pl
from jax.experimental.pallas import tpu as pltpu
from jax.sharding import PartitionSpec as P

K = 3
MESH = pl.DeviceIdType.MESH
F32 = jnp.float32
BF16 = jnp.bfloat16


def ones_where(shape, test):
    i = lax.broadcasted_iota(jnp.int32, shape, 0)
    j = lax.broadcasted_iota(jnp.int32, shape, 1)
    return jnp.where(test(i, j), 1.0, 0.0)


def nt(x, y):
    return lax.dot_general(x, y, (((1,), (1,)), ((), ())), preferred_element_type=F32)


def fold_weights(cw_ref, mw_ref, wt):
    z, zo = mw_ref.shape
    mw = mw_ref[...]
    high = mw.astype(BF16)
    low = (mw - high.astype(F32)).astype(BF16)
    spread = ones_where((4 * z, z), lambda i, j: i % z == j).astype(BF16)
    copier = ones_where((zo, K * zo), lambda i, j: j % zo == i).astype(BF16)

    def right_slot(i, j):
        slot, e = i // z, j // zo
        return ((slot == 0) & (e == 1)) | ((slot == 2) & (e == 0)) | ((slot == 3) & (e == 2))

    keep = ones_where((4 * z, K * zo), right_slot)
    parts = []
    for part in (high, low):
        tall = jnp.dot(spread, part, preferred_element_type=F32).astype(BF16)
        parts.append((jnp.dot(tall, copier, preferred_element_type=F32) * keep).astype(BF16))
    nothing = jnp.zeros((z, wt.shape[2]), BF16)
    for a in range(K):
        for b in range(K):
            at = (a * K + b) * K * zo
            rhs = cw_ref[at : at + K * zo, :]
            res = sum(jnp.dot(p, rhs, preferred_element_type=F32) for p in parts).astype(BF16)
            for f in range(2):
                for slot in range(4):
                    row = slot * 4 * z + (f + 2 - a) * z
                    wt[f * K + b, row : row + z, :] = res[slot * z : (slot + 1) * z]
    for b in range(K):
        for slot in range(4):
            row = slot * 4 * z
            wt[b, row + 3 * z : row + 4 * z, :] = nothing
            wt[K + b, row : row + z, :] = nothing


def fold_bias(mw_ref, cb_ref, mb_ref):
    z = mw_ref.shape[0]
    copier = ones_where((128, z), lambda i, j: i % z == j)
    exact = functools.partial(
        lax.dot_general, dimension_numbers=(((1,), (1,)), ((), ())),
        precision=lax.Precision.HIGHEST, preferred_element_type=F32,
    )
    return exact(exact(cb_ref[...], mw_ref[...]) + mb_ref[...], copier)


def head_kernel(
    sizes, x_hbm, cw_ref, gain_ref, mw_ref, cb_ref, mb_ref, out_ref,
    wt, xin, actf, acc, edge, pk, rs_send, ls_send, ca_send, rs_got, ls_got, ca_got, patch,
    in_sem, s1_sem, r1_sem, s2_sem, r2_sem,
):
    n_c, n_s, n_t, shard_rows = sizes
    c, s, t = lax.axis_index("cfg"), lax.axis_index("seq"), lax.axis_index("tile")
    frames, height, columns, channels = x_hbm.shape
    half = height // n_c
    pairs = half // 2
    z = 16
    chunks = pairs // shard_rows
    chunk_tokens = shard_rows * (columns // 2)

    def dev(ci, si, ti):
        return {"cfg": ci, "seq": si, "tile": ti}

    load = pltpu.make_async_copy(
        x_hbm.at[:, pl.ds(c * (half - 1), half + 1)],
        xin.at[:, pl.ds(1 - c, half + 1)],
        in_sem,
    )
    load.start()

    barrier = pltpu.get_barrier_semaphore()
    links = [(1, 0), (-1, 0), (0, 1), (1, 1), (-1, 1)]

    def there(ds, dt, sign):
        si, ti = s + sign * ds, t + sign * dt
        return (si >= 0) & (si < n_s) & (ti >= 0) & (ti < n_t), si, ti

    expect = jnp.int32(0)
    for ds, dt in links:
        ok, si, ti = there(ds, dt, -1)

        @pl.when(ok)
        def _():
            pl.semaphore_signal(barrier, inc=1, device_id=dev(c, si, ti), device_id_type=MESH)

        ok, _, _ = there(ds, dt, 1)
        expect = expect + ok.astype(jnp.int32)

    first = (s * n_t + t) * shard_rows
    src_t = first // (height // 2) // frames
    src_c = first % (height // 2) // pairs
    for si in range(n_s):
        mine = (src_c == c) & (src_t == t) & (s == si)

        @pl.when(jnp.logical_not(mine))
        def _():
            pl.semaphore_signal(barrier, inc=1, device_id=dev(src_c, si, src_t), device_id_type=MESH)

    own = (src_c == c) & (src_t == t)
    expect = expect + frames * chunks * n_c - own.astype(jnp.int32)

    fold_weights(cw_ref, mw_ref, wt)
    bias = fold_bias(mw_ref, cb_ref, mb_ref)

    zero_row = jnp.zeros((frames, 1, columns, channels), BF16)

    @pl.when(c == 0)
    def _():
        xin[:, 0:1] = zero_row

    @pl.when(c == n_c - 1)
    def _():
        xin[:, half + 1 : half + 2] = zero_row

    load.wait()
    gain = gain_ref[...]
    step_rows = 6 if (half + 2) % 6 == 0 else 2
    for f in range(frames):

        @pl.loop(0, (half + 2) // step_rows)
        def _(r):
            v = xin[f, pl.ds(r * step_rows, step_rows)].astype(F32)
            v = v.reshape(step_rows * columns, channels)
            energy = jnp.sum(v * v, axis=-1, keepdims=True) * (1.0 / channels)
            v = v * lax.rsqrt(energy + 1e-06) * gain
            v = v / (1.0 + jnp.exp(-v))
            at = pl.multiple_of(r * (step_rows * columns), step_rows * columns)
            actf[f, pl.ds(at, step_rows * columns), :] = v

    rows = half * columns
    for m in range(2):
        lo = m * (rows // 2)
        total = None
        for f in range(frames):
            for b in range(K):
                lhs = actf[f, lo + b * columns : lo + b * columns + rows // 2, :].astype(BF16)
                term = nt(lhs, wt[f * K + b])
                total = term if total is None else total + term
        acc[lo : lo + rows // 2, :] = total[:, :128]
        edge[lo : lo + rows // 2, :] = total[:, 128:]

    q = edge[...]
    w_at = lax.broadcasted_iota(jnp.int32, (rows, 128), 0) % columns
    right = jnp.where(w_at == 0, 0.0, pltpu.roll(q, 1, 0))
    left = jnp.where(w_at == columns - 1, 0.0, pltpu.roll(q, rows - 1, 0))
    acc[...] = acc[...] + right + pltpu.roll(left, 64, 1)
    rs_send[...] = edge[pl.ds(columns - 1, half, stride=columns), :].astype(BF16)
    ls_send[...] = edge[pl.ds(0, half, stride=columns), :].astype(BF16)
    quarter = rows // 4
    lane = lax.broadcasted_iota(jnp.int32, (quarter, 128), 1)
    packed = jnp.zeros((quarter, 128), F32)
    for k in range(4):
        part = pltpu.roll(acc[k * quarter : (k + 1) * quarter, :], (k * 32 + 128 - 32) % 128, 1)
        packed = jnp.where(lane // 32 == k, part, packed)
    ca_send[...] = packed.astype(BF16)

    pl.semaphore_wait(barrier, expect)

    bufs = {1: (rs_send, rs_got), -1: (ls_send, ls_got), 0: (ca_send, ca_got)}

    def link_copy(i, sign):
        ds, dt = links[i]
        ok, si, ti = there(ds, dt, sign)
        src, dst = bufs[ds]
        if ds != 0:
            dst = dst.at[dt]
        return ok, pltpu.make_async_remote_copy(
            src_ref=src, dst_ref=dst, send_sem=s1_sem.at[i], recv_sem=r1_sem.at[i],
            device_id=dev(c, si, ti), device_id_type=MESH,
        )

    for i in (2, 3, 4, 0, 1):
        ok, copy = link_copy(i, 1)

        @pl.when(ok)
        def _():
            copy.start()

    for i in (0, 1, 3, 4, 2):
        ds, dt = links[i]
        ok, copy = link_copy(i, -1)

        @pl.when(ok)
        def _():
            copy.wait_recv()
            if ds == 0:
                got = ca_got[...].astype(F32)
                for k in range(4):
                    acc[k * quarter : (k + 1) * quarter, :] += pltpu.roll(got, (128 - 32 * k) % 128, 1)
            else:
                got = bufs[ds][1][dt].astype(F32)
                turn = (128 - 32 * dt - (64 if ds < 0 else 0)) % 128
                if turn:
                    got = pltpu.roll(got, turn, 1)
                at = pl.ds(0 if ds > 0 else columns - 1, half, stride=columns)
                acc[at, :] = acc[at, :] + got

    total = acc[...] + bias
    by_row = total.reshape(pairs, 2, columns, 128)
    even = by_row[:, 0].reshape(pairs * columns, 128)
    odd = by_row[:, 1].reshape(pairs * columns, 128)
    lane = lax.broadcasted_iota(jnp.int32, (pairs * columns, 128), 1)
    mixed = jnp.where(
        lane < 16, even,
        jnp.where(
            lane < 32, pltpu.roll(odd, 16, 1),
            jnp.where(lane < 48, pltpu.roll(even, 16, 1), pltpu.roll(odd, 32, 1)),
        ),
    )
    pk[...] = mixed
    tokens = pairs * columns // 2
    left_half = pk[pl.ds(0, tokens, stride=2), :]
    right_half = pk[pl.ds(1, tokens, stride=2), :]
    lane = lax.broadcasted_iota(jnp.int32, (tokens, 128), 1)
    for f in range(frames):
        one = left_half if f == 0 else pltpu.roll(left_half, 128 - 32 * f, 1)
        two = pltpu.roll(right_half, (32 - 32 * f) % 128, 1) if f != 1 else right_half
        both = jnp.where(lane < 32, one, two)
        for m in range(chunks):
            patch[f * chunks + m] = both[m * chunk_tokens : (m + 1) * chunk_tokens, :64].astype(BF16)

    def patch_copy(f, m, ci):
        shard = ((t * frames + f) * (height // 2) + c * pairs) // shard_rows + m
        si, ti = shard // n_t, shard % n_t
        mine = (si == s) & (ti == t) & (c == ci)
        piece = f * chunks + m
        local = pltpu.make_async_copy(patch.at[piece], out_ref.at[s], r2_sem.at[s])
        away = pltpu.make_async_remote_copy(
            src_ref=patch.at[piece], dst_ref=out_ref.at[s],
            send_sem=s2_sem.at[piece * n_c + ci], recv_sem=r2_sem.at[s],
            device_id=dev(ci, si, ti), device_id_type=MESH,
        )
        return mine, local, away

    every = [(f, m, ci) for f in range(frames) for m in range(chunks) for ci in range(n_c)]
    for item in every:
        mine, local, away = patch_copy(*item)

        @pl.when(mine)
        def _():
            local.start()

        @pl.when(jnp.logical_not(mine))
        def _():
            away.start()

    for si in range(n_s):
        pltpu.make_async_copy(patch.at[0], out_ref.at[si], r2_sem.at[si]).wait()
    for i in range(5):
        ok, copy = link_copy(i, 1)

        @pl.when(ok)
        def _():
            copy.wait_send()

    for item in every:
        mine, _, away = patch_copy(*item)

        @pl.when(jnp.logical_not(mine))
        def _():
            away.wait_send()


def tail_kernel(noisy, mask, lat, pw, cw, pb, cb, shift, scale, out, comb, both, sems):
    split = lat.shape[-1]
    width = comb.shape[1]
    step = 512
    z = split // 4

    @pl.when(pl.program_id(0) == 0)
    def _():
        upper = pltpu.make_async_copy(pw, both.at[:split], sems.at[0])
        lower = pltpu.make_async_copy(cw, both.at[split:], sems.at[1])
        upper.start()
        lower.start()
        upper.wait()
        lower.wait()

    perm = ones_where(
        (split, split), lambda i, j: j == (i % z) * 4 + (i // z % 2) * 2 + i // (2 * z)
    ).astype(BF16)
    if len(lat.shape) == 3:
        strips, per, _ = lat.shape
        tokens = lat[...].reshape(strips * per, split)
        n, cols = strips * per, 4
        order = ones_where(
            (n, n),
            lambda i, j: j == (i // cols % strips) * per + i // (cols * strips) * cols + i % cols,
        ).astype(BF16)
        tokens = jnp.dot(order, tokens, preferred_element_type=F32).astype(BF16)
    else:
        tokens = lat[...]
    tokens = jnp.dot(tokens, perm, preferred_element_type=F32)
    own = noisy[...].astype(F32).T
    lhs = jnp.concatenate([own, tokens, mask[...].astype(F32)], axis=1).astype(BF16)
    total = None
    for k in range(0, width, step):
        at = slice(k, k + step)
        part = jnp.dot(lhs, both[:, at], preferred_element_type=F32)
        part = part + (pb[:, at] + cb[:, at])
        comb[:, at] = part
        term = jnp.sum(part, axis=-1, keepdims=True)
        total = term if total is None else total + term
    mean = total * (1.0 / width)
    square = None
    for k in range(0, width, step):
        d = comb[:, k : k + step] - mean
        term = jnp.sum(d * d, axis=-1, keepdims=True)
        square = term if square is None else square + term
    inv = lax.rsqrt(square * (1.0 / width) + 1e-06)
    for k in range(0, width, step):
        at = slice(k, k + step)
        out[:, at] = ((comb[:, at] - mean) * inv * (1.0 + scale[:, at]) + shift[:, at]).astype(BF16)


def body(
    section_input, norm_gain, conv_weight, conv_bias, mean_weight, mean_bias, noisy_tokens,
    mask_tokens, patch_weight, patch_bias, context_weight, context_bias, norm_shift, norm_scale,
):
    frames, height, columns, channels = section_input.shape
    n_c, n_s, n_t = lax.axis_size("cfg"), lax.axis_size("seq"), lax.axis_size("tile")
    z = mean_weight.shape[1]
    tokens = noisy_tokens.shape[0]
    shard_rows = tokens // (n_s * columns // 2)
    half = height // n_c
    rows = half * columns
    chunks = half // 2 // shard_rows
    chunk_tokens = shard_rows * (columns // 2)
    vmem = pl.BlockSpec(memory_space=pltpu.VMEM)
    arrived = pl.pallas_call(
        functools.partial(head_kernel, (n_c, n_s, n_t, shard_rows)),
        out_shape=jax.ShapeDtypeStruct((n_s, chunk_tokens, 4 * z), BF16),
        in_specs=[pl.BlockSpec(memory_space=pl.ANY)] + [vmem] * 5,
        out_specs=vmem,
        scratch_shapes=[
            pltpu.VMEM((frames * K, 16 * z, channels), BF16),
            pltpu.VMEM((frames, half + 2, columns, channels), BF16),
            pltpu.VMEM((frames, (half + 2) * columns, channels), F32),
            pltpu.VMEM((rows, 128), F32),
            pltpu.VMEM((rows, 128), F32),
            pltpu.VMEM((rows // 2, 128), F32),
            pltpu.VMEM((half, 128), BF16),
            pltpu.VMEM((half, 128), BF16),
            pltpu.VMEM((rows // 4, 128), BF16),
            pltpu.VMEM((2, half, 128), BF16),
            pltpu.VMEM((2, half, 128), BF16),
            pltpu.VMEM((rows // 4, 128), BF16),
            pltpu.VMEM((frames * chunks, chunk_tokens, 4 * z), BF16),
            pltpu.SemaphoreType.DMA,
            pltpu.SemaphoreType.DMA((5,)),
            pltpu.SemaphoreType.DMA((5,)),
            pltpu.SemaphoreType.DMA((frames * chunks * n_c,)),
            pltpu.SemaphoreType.DMA((n_s,)),
        ],
        compiler_params=pltpu.CompilerParams(collective_id=0, has_side_effects=True),
        name="head",
    )(
        section_input, conv_weight.T, norm_gain[None], mean_weight.T, conv_bias[None], mean_bias[None]
    )
    width = patch_weight.shape[1]
    block = min(tokens, 256)
    per = block // n_s
    if per % 16 == 0 and columns == 8:
        lat = arrived
        lat_spec = pl.BlockSpec((n_s, per, 4 * z), lambda i: (0, i, 0))
    else:
        lat = arrived.reshape(n_s, shard_rows, columns // 2, 4 * z).transpose(1, 0, 2, 3)
        lat = lat.reshape(tokens, 4 * z)
        lat_spec = pl.BlockSpec((block, 4 * z), lambda i: (i, 0))
    tok = lambda n: pl.BlockSpec((block, n), lambda i: (i, 0))
    full = lambda a: pl.BlockSpec(a.shape, lambda i: (0, 0))
    hbm = pl.BlockSpec(memory_space=pl.ANY)
    depth = patch_weight.shape[0] + context_weight.shape[0]
    vecs = [v[None] for v in (patch_bias, context_bias, norm_shift, norm_scale)]
    return pl.pallas_call(
        tail_kernel,
        out_shape=jax.ShapeDtypeStruct((tokens, width), BF16),
        grid=(tokens // block,),
        in_specs=[
            pl.BlockSpec((noisy_tokens.shape[1], block), lambda i: (0, i)),
            tok(mask_tokens.shape[1]), lat_spec, hbm, hbm,
        ]
        + [full(v) for v in vecs],
        out_specs=tok(width),
        scratch_shapes=[
            pltpu.VMEM((block, width), F32),
            pltpu.VMEM((depth, width), BF16),
            pltpu.SemaphoreType.DMA((2,)),
        ],
        name="tail",
    )(noisy_tokens.T, mask_tokens, lat, patch_weight, context_weight, *vecs)


def solution(mesh):
    placed = (P("tile", None, "seq", None),) + (P(),) * 5
    placed = placed + (P(("seq", "tile"), None),) * 2 + (P(),) * 6
    return jax.shard_map(
        body, mesh=mesh, in_specs=placed, out_specs=P(("seq", "tile"), None), check_vma=False
    )
```

```python
import functools

import jax
import jax.numpy as jnp
from jax import lax
from jax.experimental import pallas as pl
from jax.experimental.pallas import tpu as pltpu
from jax.sharding import PartitionSpec as P

K = 3
MESH = pl.DeviceIdType.MESH
F32 = jnp.float32
BF16 = jnp.bfloat16


def ones_where(shape, test):
    i = lax.broadcasted_iota(jnp.int32, shape, 0)
    j = lax.broadcasted_iota(jnp.int32, shape, 1)
    return jnp.where(test(i, j), 1.0, 0.0)


def nt(x, y):
    return lax.dot_general(x, y, (((1,), (1,)), ((), ())), preferred_element_type=F32)


def fold_weights(cw_ref, mw_ref, wt):
    z, zo = mw_ref.shape
    mw = mw_ref[...]
    high = mw.astype(BF16)
    low = (mw - high.astype(F32)).astype(BF16)
    spread = ones_where((4 * z, z), lambda i, j: i % z == j).astype(BF16)
    copier = ones_where((zo, K * zo), lambda i, j: j % zo == i).astype(BF16)

    def right_slot(i, j):
        slot, e = i // z, j // zo
        return ((slot == 0) & (e == 1)) | ((slot == 2) & (e == 0)) | ((slot == 3) & (e == 2))

    keep = ones_where((4 * z, K * zo), right_slot)
    parts = []
    for part in (high, low):
        tall = jnp.dot(spread, part, preferred_element_type=F32).astype(BF16)
        parts.append((jnp.dot(tall, copier, preferred_element_type=F32) * keep).astype(BF16))
    parts = jnp.concatenate(parts, axis=0)
    nothing = jnp.zeros((z, wt.shape[2]), BF16)
    for a in range(K):
        for b in range(K):
            at = (a * K + b) * K * zo
            rhs = cw_ref[at : at + K * zo, :]
            res = jnp.dot(parts, rhs, preferred_element_type=F32)
            res = (res[: 4 * z] + res[4 * z :]).astype(BF16)
            for f in range(2):
                for slot in range(4):
                    row = slot * 4 * z + (f + 2 - a) * z
                    wt[f * K + b, row : row + z, :] = res[slot * z : (slot + 1) * z]
    for b in range(K):
        for slot in range(4):
            row = slot * 4 * z
            wt[b, row + 3 * z : row + 4 * z, :] = nothing
            wt[K + b, row : row + z, :] = nothing


def fold_bias(mw_ref, cb_ref, mb_ref):
    z = mw_ref.shape[0]
    copier = ones_where((128, z), lambda i, j: i % z == j)
    exact = functools.partial(
        lax.dot_general, dimension_numbers=(((1,), (1,)), ((), ())),
        precision=lax.Precision.HIGHEST, preferred_element_type=F32,
    )
    return exact(exact(cb_ref[...], mw_ref[...]) + mb_ref[...], copier)


def head_kernel(
    sizes, x_hbm, cw_ref, gain_ref, mw_ref, cb_ref, mb_ref, out_ref,
    wt, xin, actf, acc, edge, pk, rs_send, ls_send, ca_send, rs_got, ls_got, ca_got, patch,
    in_sem, s1_sem, r1_sem, s2_sem, r2_sem,
):
    n_c, n_s, n_t, shard_rows = sizes
    c, s, t = lax.axis_index("cfg"), lax.axis_index("seq"), lax.axis_index("tile")
    frames, height, columns, channels = x_hbm.shape
    half = height // n_c
    pairs = half // 2
    z = 16
    chunks = pairs // shard_rows
    chunk_tokens = shard_rows * (columns // 2)

    def dev(ci, si, ti):
        return {"cfg": ci, "seq": si, "tile": ti}

    load = pltpu.make_async_copy(
        x_hbm.at[:, pl.ds(c * (half - 1), half + 1)],
        xin.at[:, pl.ds(1 - c, half + 1)],
        in_sem,
    )
    load.start()

    barrier = pltpu.get_barrier_semaphore()
    links = [(1, 0), (-1, 0), (0, 1), (1, 1), (-1, 1)]

    def there(ds, dt, sign):
        si, ti = s + sign * ds, t + sign * dt
        return (si >= 0) & (si < n_s) & (ti >= 0) & (ti < n_t), si, ti

    expect = jnp.int32(0)
    for ds, dt in links:
        ok, si, ti = there(ds, dt, -1)

        @pl.when(ok)
        def _():
            pl.semaphore_signal(barrier, inc=1, device_id=dev(c, si, ti), device_id_type=MESH)

        ok, _, _ = there(ds, dt, 1)
        expect = expect + ok.astype(jnp.int32)

    first = (s * n_t + t) * shard_rows
    src_t = first // (height // 2) // frames
    src_c = first % (height // 2) // pairs
    for si in range(n_s):
        mine = (src_c == c) & (src_t == t) & (s == si)

        @pl.when(jnp.logical_not(mine))
        def _():
            pl.semaphore_signal(barrier, inc=1, device_id=dev(src_c, si, src_t), device_id_type=MESH)

    own = (src_c == c) & (src_t == t)
    expect = expect + frames * chunks * n_c - own.astype(jnp.int32)

    fold_weights(cw_ref, mw_ref, wt)
    bias = fold_bias(mw_ref, cb_ref, mb_ref)

    zero_row = jnp.zeros((frames, 1, columns, channels), BF16)

    @pl.when(c == 0)
    def _():
        xin[:, 0:1] = zero_row

    @pl.when(c == n_c - 1)
    def _():
        xin[:, half + 1 : half + 2] = zero_row

    load.wait()
    gain = gain_ref[...].reshape(1, channels)
    step_rows = 6 if (half + 2) % 6 == 0 else 2
    for f in range(frames):

        @pl.loop(0, (half + 2) // step_rows)
        def _(r):
            v = xin[f, pl.ds(r * step_rows, step_rows)].astype(F32)
            v = v.reshape(step_rows * columns, channels)
            energy = jnp.sum(v * v, axis=-1, keepdims=True) * (1.0 / channels)
            v = v * lax.rsqrt(energy + 1e-06) * gain
            v = v / (1.0 + jnp.exp(-v))
            at = pl.multiple_of(r * (step_rows * columns), step_rows * columns)
            actf[f, pl.ds(at, step_rows * columns), :] = v

    rows = half * columns
    for m in range(2):
        lo = m * (rows // 2)
        total = None
        for f in range(frames):
            for b in range(K):
                lhs = actf[f, lo + b * columns : lo + b * columns + rows // 2, :].astype(BF16)
                term = nt(lhs, wt[f * K + b])
                total = term if total is None else total + term
        acc[lo : lo + rows // 2, :] = total[:, :128]
        edge[lo : lo + rows // 2, :] = total[:, 128:]

    q = edge[...]
    w_at = lax.broadcasted_iota(jnp.int32, (rows, 128), 0) % columns
    right = jnp.where(w_at == 0, 0.0, pltpu.roll(q, 1, 0))
    left = jnp.where(w_at == columns - 1, 0.0, pltpu.roll(q, rows - 1, 0))
    acc[...] = acc[...] + right + pltpu.roll(left, 64, 1)
    rs_send[...] = edge[pl.ds(columns - 1, half, stride=columns), :].astype(BF16)
    ls_send[...] = edge[pl.ds(0, half, stride=columns), :].astype(BF16)
    quarter = rows // 4
    lane = lax.broadcasted_iota(jnp.int32, (quarter, 128), 1)
    packed = jnp.zeros((quarter, 128), F32)
    for k in range(4):
        part = pltpu.roll(acc[k * quarter : (k + 1) * quarter, :], (k * 32 + 128 - 32) % 128, 1)
        packed = jnp.where(lane // 32 == k, part, packed)
    ca_send[...] = packed.astype(BF16)

    pl.semaphore_wait(barrier, expect)

    bufs = {1: (rs_send, rs_got), -1: (ls_send, ls_got), 0: (ca_send, ca_got)}

    def link_copy(i, sign):
        ds, dt = links[i]
        ok, si, ti = there(ds, dt, sign)
        src, dst = bufs[ds]
        if ds != 0:
            dst = dst.at[dt]
        return ok, pltpu.make_async_remote_copy(
            src_ref=src, dst_ref=dst, send_sem=s1_sem.at[i], recv_sem=r1_sem.at[i],
            device_id=dev(c, si, ti), device_id_type=MESH,
        )

    for i in (2, 3, 4, 0, 1):
        ok, copy = link_copy(i, 1)

        @pl.when(ok)
        def _():
            copy.start()

    for i in (0, 1, 3, 4, 2):
        ds, dt = links[i]
        ok, copy = link_copy(i, -1)

        @pl.when(ok)
        def _():
            copy.wait_recv()
            if ds == 0:
                got = ca_got[...].astype(F32)
                for k in range(4):
                    acc[k * quarter : (k + 1) * quarter, :] += pltpu.roll(got, (128 - 32 * k) % 128, 1)
            else:
                got = bufs[ds][1][dt].astype(F32)
                turn = (128 - 32 * dt - (64 if ds < 0 else 0)) % 128
                if turn:
                    got = pltpu.roll(got, turn, 1)
                at = pl.ds(0 if ds > 0 else columns - 1, half, stride=columns)
                acc[at, :] = acc[at, :] + got

    total = acc[...] + bias
    by_row = total.reshape(pairs, 2, columns, 128)
    even = by_row[:, 0].reshape(pairs * columns, 128)
    odd = by_row[:, 1].reshape(pairs * columns, 128)
    lane = lax.broadcasted_iota(jnp.int32, (pairs * columns, 128), 1)
    mixed = jnp.where(
        lane < 16, even,
        jnp.where(
            lane < 32, pltpu.roll(odd, 16, 1),
            jnp.where(lane < 48, pltpu.roll(even, 16, 1), pltpu.roll(odd, 32, 1)),
        ),
    )
    pk[...] = mixed
    tokens = pairs * columns // 2
    left_half = pk[pl.ds(0, tokens, stride=2), :]
    right_half = pk[pl.ds(1, tokens, stride=2), :]
    lane = lax.broadcasted_iota(jnp.int32, (tokens, 128), 1)
    for f in range(frames):
        one = left_half if f == 0 else pltpu.roll(left_half, 128 - 32 * f, 1)
        two = pltpu.roll(right_half, (32 - 32 * f) % 128, 1) if f != 1 else right_half
        both = jnp.where(lane < 32, one, two)
        for m in range(chunks):
            patch[f * chunks + m] = both[m * chunk_tokens : (m + 1) * chunk_tokens, :64].astype(BF16)

    def patch_copy(f, m, ci):
        shard = ((t * frames + f) * (height // 2) + c * pairs) // shard_rows + m
        si, ti = shard // n_t, shard % n_t
        mine = (si == s) & (ti == t) & (c == ci)
        piece = f * chunks + m
        local = pltpu.make_async_copy(patch.at[piece], out_ref.at[s], r2_sem.at[s])
        away = pltpu.make_async_remote_copy(
            src_ref=patch.at[piece], dst_ref=out_ref.at[s],
            send_sem=s2_sem.at[piece * n_c + ci], recv_sem=r2_sem.at[s],
            device_id=dev(ci, si, ti), device_id_type=MESH,
        )
        return mine, local, away

    every = [(f, m, ci) for f in range(frames) for m in range(chunks) for ci in range(n_c)]
    for item in every:
        mine, local, away = patch_copy(*item)

        @pl.when(mine)
        def _():
            local.start()

        @pl.when(jnp.logical_not(mine))
        def _():
            away.start()

    for si in range(n_s):
        pltpu.make_async_copy(patch.at[0], out_ref.at[si], r2_sem.at[si]).wait()
    for i in range(5):
        ok, copy = link_copy(i, 1)

        @pl.when(ok)
        def _():
            copy.wait_send()

    for item in every:
        mine, _, away = patch_copy(*item)

        @pl.when(jnp.logical_not(mine))
        def _():
            away.wait_send()


def tail_kernel(noisy, mask, lat, pw, cw, pb, cb, shift, scale, out, comb, both, inv_ref, mean_ref, sems):
    split = lat.shape[-1]
    width = comb.shape[1]
    step = 512
    z = split // 4

    @pl.when(pl.program_id(0) == 0)
    def _():
        upper = pltpu.make_async_copy(pw, both.at[:split], sems.at[0])
        lower = pltpu.make_async_copy(cw, both.at[split:], sems.at[1])
        upper.start()
        lower.start()
        upper.wait()
        lower.wait()

    parts = comb.shape[0] // out.shape[0]

    @pl.when(pl.program_id(0) % parts == 0)
    def _():
        perm = ones_where(
            (split, split), lambda i, j: j == (i % z) * 4 + (i // z % 2) * 2 + i // (2 * z)
        ).astype(BF16)
        if len(lat.shape) == 3:
            strips, per, _ = lat.shape
            tokens = lat[...].reshape(strips * per, split)
            n, cols = strips * per, 4
            order = ones_where(
                (n, n),
                lambda i, j: j == (i // cols % strips) * per + i // (cols * strips) * cols + i % cols,
            ).astype(BF16)
            tokens = jnp.dot(order, tokens, preferred_element_type=F32).astype(BF16)
        else:
            tokens = lat[...]
        tokens = jnp.dot(tokens, perm, preferred_element_type=F32)
        own = noisy[...].astype(F32).T
        lhs = jnp.concatenate([own, tokens, mask[...].astype(F32)], axis=1).astype(BF16)
        total = None
        for k in range(0, width, step):
            at = slice(k, k + step)
            part = jnp.dot(lhs, both[:, at], preferred_element_type=F32)
            part = part + (pb[:, at] + cb[:, at])
            comb[:, at] = part
            term = jnp.sum(part, axis=-1, keepdims=True)
            total = term if total is None else total + term
        mean = total * (1.0 / width)
        square = None
        for k in range(0, width, step):
            d = comb[:, k : k + step] - mean
            term = jnp.sum(d * d, axis=-1, keepdims=True)
            square = term if square is None else square + term
        mean_ref[...] = jnp.broadcast_to(mean, mean_ref.shape)
        inv_ref[...] = jnp.broadcast_to(lax.rsqrt(square * (1.0 / width) + 1e-06), inv_ref.shape)

    rows = out.shape[0]
    mine = pl.ds(pl.multiple_of(pl.program_id(0) % parts * rows, rows), rows)
    mean, inv = mean_ref[mine, :1], inv_ref[mine, :1]
    for k in range(0, width, step):
        at = slice(k, k + step)
        out[:, at] = ((comb[mine, at] - mean) * inv * (1.0 + scale[:, at]) + shift[:, at]).astype(BF16)


def body(
    section_input, norm_gain, conv_weight, conv_bias, mean_weight, mean_bias, noisy_tokens,
    mask_tokens, patch_weight, patch_bias, context_weight, context_bias, norm_shift, norm_scale,
):
    frames, height, columns, channels = section_input.shape
    n_c, n_s, n_t = lax.axis_size("cfg"), lax.axis_size("seq"), lax.axis_size("tile")
    z = mean_weight.shape[1]
    tokens = noisy_tokens.shape[0]
    shard_rows = tokens // (n_s * columns // 2)
    half = height // n_c
    rows = half * columns
    chunks = half // 2 // shard_rows
    chunk_tokens = shard_rows * (columns // 2)
    vmem = pl.BlockSpec(memory_space=pltpu.VMEM)
    arrived = pl.pallas_call(
        functools.partial(head_kernel, (n_c, n_s, n_t, shard_rows)),
        out_shape=jax.ShapeDtypeStruct((n_s, chunk_tokens, 4 * z), BF16),
        in_specs=[pl.BlockSpec(memory_space=pltpu.HBM)] + [vmem] * 5,
        out_specs=vmem,
        scratch_shapes=[
            pltpu.VMEM((frames * K, 16 * z, channels), BF16),
            pltpu.VMEM((frames, half + 2, columns, channels), BF16),
            pltpu.VMEM((frames, (half + 2) * columns, channels), F32),
            pltpu.VMEM((rows, 128), F32),
            pltpu.VMEM((rows, 128), F32),
            pltpu.VMEM((rows // 2, 128), F32),
            pltpu.VMEM((half, 128), BF16),
            pltpu.VMEM((half, 128), BF16),
            pltpu.VMEM((rows // 4, 128), BF16),
            pltpu.VMEM((2, half, 128), BF16),
            pltpu.VMEM((2, half, 128), BF16),
            pltpu.VMEM((rows // 4, 128), BF16),
            pltpu.VMEM((frames * chunks, chunk_tokens, 4 * z), BF16),
            pltpu.SemaphoreType.DMA,
            pltpu.SemaphoreType.DMA((5,)),
            pltpu.SemaphoreType.DMA((5,)),
            pltpu.SemaphoreType.DMA((frames * chunks * n_c,)),
            pltpu.SemaphoreType.DMA((n_s,)),
        ],
        compiler_params=pltpu.CompilerParams(
            collective_id=0, has_side_effects=True, vmem_limit_bytes=20 * 2**20
        ),
        name="head",
    )(
        section_input, conv_weight.T, norm_gain, mean_weight.T, conv_bias[None], mean_bias[None]
    )
    width = patch_weight.shape[1]
    block = min(tokens, 256)
    per = block // n_s
    if per % 16 == 0 and columns == 8:
        lat = arrived
        lat_spec = pl.BlockSpec((n_s, per, 4 * z), lambda i: (0, i // parts, 0))
    else:
        lat = arrived.reshape(n_s, shard_rows, columns // 2, 4 * z).transpose(1, 0, 2, 3)
        lat = lat.reshape(tokens, 4 * z)
        lat_spec = pl.BlockSpec((block, 4 * z), lambda i: (i // parts, 0))
    parts = 2 if block % 32 == 0 else 1
    tok = lambda n: pl.BlockSpec((block, n), lambda i: (i // parts, 0))
    full = lambda a: pl.BlockSpec(a.shape, lambda i: (0, 0))
    hbm = pl.BlockSpec(memory_space=pl.ANY)
    depth = patch_weight.shape[0] + context_weight.shape[0]
    vecs = [v[None] for v in (patch_bias, context_bias, norm_shift, norm_scale)]
    return pl.pallas_call(
        tail_kernel,
        out_shape=jax.ShapeDtypeStruct((tokens, width), BF16),
        grid=(tokens // block * parts,),
        in_specs=[
            pl.BlockSpec((noisy_tokens.shape[1], block), lambda i: (0, i // parts)),
            tok(mask_tokens.shape[1]), lat_spec, hbm, hbm,
        ]
        + [full(v) for v in vecs],
        out_specs=pl.BlockSpec((block // parts, width), lambda i: (i, 0)),
        scratch_shapes=[
            pltpu.VMEM((block, width), F32),
            pltpu.VMEM((depth, width), BF16),
            pltpu.VMEM((block, 128), F32),
            pltpu.VMEM((block, 128), F32),
            pltpu.SemaphoreType.DMA((2,)),
        ],
        compiler_params=pltpu.CompilerParams(vmem_limit_bytes=28 * 2**20),
        name="tail",
    )(noisy_tokens.T, mask_tokens, lat, patch_weight, context_weight, *vecs)


def solution(mesh):
    placed = (P("tile", None, "seq", None),) + (P(),) * 5
    placed = placed + (P(("seq", "tile"), None),) * 2 + (P(),) * 6
    return jax.shard_map(
        body, mesh=mesh, in_specs=placed, out_specs=P(("seq", "tile"), None), check_vma=False
    )
```

```python
import functools

import jax
import jax.numpy as jnp
from jax import lax
from jax.experimental import pallas as pl
from jax.experimental.pallas import tpu as pltpu
from jax.sharding import PartitionSpec as P

K = 3
MESH = pl.DeviceIdType.MESH
F32 = jnp.float32
BF16 = jnp.bfloat16


def ones_where(shape, test):
    i = lax.broadcasted_iota(jnp.int32, shape, 0)
    j = lax.broadcasted_iota(jnp.int32, shape, 1)
    return jnp.where(test(i, j), 1.0, 0.0)


def nt(x, y):
    return lax.dot_general(x, y, (((1,), (1,)), ((), ())), preferred_element_type=F32)


def fold_weights(cw_ref, mw_ref, wt):
    z, zo = mw_ref.shape
    mw = mw_ref[...]
    high = mw.astype(BF16)
    low = (mw - high.astype(F32)).astype(BF16)
    spread = ones_where((4 * z, z), lambda i, j: i % z == j).astype(BF16)
    copier = ones_where((zo, K * zo), lambda i, j: j % zo == i).astype(BF16)

    def right_slot(i, j):
        slot, e = i // z, j // zo
        return ((slot == 0) & (e == 1)) | ((slot == 2) & (e == 0)) | ((slot == 3) & (e == 2))

    keep = ones_where((4 * z, K * zo), right_slot)
    parts = []
    for part in (high, low):
        tall = jnp.dot(spread, part, preferred_element_type=F32).astype(BF16)
        parts.append((jnp.dot(tall, copier, preferred_element_type=F32) * keep).astype(BF16))
    parts = jnp.concatenate(parts, axis=0)
    nothing = jnp.zeros((z, wt.shape[2]), BF16)
    for a in range(K):
        for b in range(K):
            at = (a * K + b) * K * zo
            rhs = cw_ref[at : at + K * zo, :]
            res = jnp.dot(parts, rhs, preferred_element_type=F32)
            res = (res[: 4 * z] + res[4 * z :]).astype(BF16)
            for f in range(2):
                for slot in range(4):
                    row = slot * 4 * z + (f + 2 - a) * z
                    wt[f * K + b, row : row + z, :] = res[slot * z : (slot + 1) * z]
    for b in range(K):
        for slot in range(4):
            row = slot * 4 * z
            wt[b, row + 3 * z : row + 4 * z, :] = nothing
            wt[K + b, row : row + z, :] = nothing


def fold_bias(mw_ref, cb_ref, mb_ref):
    z = mw_ref.shape[0]
    copier = ones_where((128, z), lambda i, j: i % z == j)
    exact = functools.partial(
        lax.dot_general, dimension_numbers=(((1,), (1,)), ((), ())),
        precision=lax.Precision.HIGHEST, preferred_element_type=F32,
    )
    return exact(exact(cb_ref[...], mw_ref[...]) + mb_ref[...], copier)


def head_kernel(
    sizes, x_hbm, cw_ref, gain_ref, mw_ref, cb_ref, mb_ref, out_ref,
    wt, xin, actf, acc, edge, pk, rs_send, ls_send, ca_send, rs_got, ls_got, ca_got, patch,
    in_sem, s1_sem, r1_sem, s2_sem, r2_sem,
):
    n_c, n_s, n_t, shard_rows = sizes
    c, s, t = lax.axis_index("cfg"), lax.axis_index("seq"), lax.axis_index("tile")
    frames, height, columns, channels = x_hbm.shape
    half = height // n_c
    pairs = half // 2
    z = 16
    chunks = pairs // shard_rows
    chunk_tokens = shard_rows * (columns // 2)

    def dev(ci, si, ti):
        return {"cfg": ci, "seq": si, "tile": ti}

    load = pltpu.make_async_copy(
        x_hbm.at[:, pl.ds(c * (half - 1), half + 1)],
        xin.at[:, pl.ds(1 - c, half + 1)],
        in_sem,
    )
    load.start()

    barrier = pltpu.get_barrier_semaphore()
    links = [(1, 0), (-1, 0), (0, 1), (1, 1), (-1, 1)]

    def there(ds, dt, sign):
        si, ti = s + sign * ds, t + sign * dt
        return (si >= 0) & (si < n_s) & (ti >= 0) & (ti < n_t), si, ti

    expect = jnp.int32(0)
    for ds, dt in links:
        ok, si, ti = there(ds, dt, -1)

        @pl.when(ok)
        def _():
            pl.semaphore_signal(barrier, inc=1, device_id=dev(c, si, ti), device_id_type=MESH)

        ok, _, _ = there(ds, dt, 1)
        expect = expect + ok.astype(jnp.int32)

    first = (s * n_t + t) * shard_rows
    src_t = first // (height // 2) // frames
    src_c = first % (height // 2) // pairs
    for si in range(n_s):
        mine = (src_c == c) & (src_t == t) & (s == si)

        @pl.when(jnp.logical_not(mine))
        def _():
            pl.semaphore_signal(barrier, inc=1, device_id=dev(src_c, si, src_t), device_id_type=MESH)

    own = (src_c == c) & (src_t == t)
    expect = expect + frames * chunks * n_c - own.astype(jnp.int32)

    fold_weights(cw_ref, mw_ref, wt)
    bias = fold_bias(mw_ref, cb_ref, mb_ref)

    zero_row = jnp.zeros((frames, 1, columns, channels), BF16)

    @pl.when(c == 0)
    def _():
        xin[:, 0:1] = zero_row

    @pl.when(c == n_c - 1)
    def _():
        xin[:, half + 1 : half + 2] = zero_row

    load.wait()
    gain = gain_ref[...].reshape(1, channels)
    step_rows = 6 if (half + 2) % 6 == 0 else 2
    for f in range(frames):

        @pl.loop(0, (half + 2) // step_rows)
        def _(r):
            v = xin[f, pl.ds(r * step_rows, step_rows)].astype(F32)
            v = v.reshape(step_rows * columns, channels)
            energy = jnp.sum(v * v, axis=-1, keepdims=True) * (1.0 / channels)
            v = v * lax.rsqrt(energy + 1e-06) * gain
            v = v / (1.0 + jnp.exp(-v))
            at = pl.multiple_of(r * (step_rows * columns), step_rows * columns)
            actf[f, pl.ds(at, step_rows * columns), :] = v

    rows = half * columns
    for m in range(2):
        lo = m * (rows // 2)
        total = None
        for f in range(frames):
            for b in range(K):
                lhs = actf[f, lo + b * columns : lo + b * columns + rows // 2, :].astype(BF16)
                term = nt(lhs, wt[f * K + b])
                total = term if total is None else total + term
        acc[lo : lo + rows // 2, :] = total[:, :128]
        edge[lo : lo + rows // 2, :] = total[:, 128:]

    q = edge[...]
    w_at = lax.broadcasted_iota(jnp.int32, (rows, 128), 0) % columns
    right = jnp.where(w_at == 0, 0.0, pltpu.roll(q, 1, 0))
    left = jnp.where(w_at == columns - 1, 0.0, pltpu.roll(q, rows - 1, 0))
    acc[...] = acc[...] + right + pltpu.roll(left, 64, 1)
    rs_send[...] = edge[pl.ds(columns - 1, half, stride=columns), :].astype(BF16)
    ls_send[...] = edge[pl.ds(0, half, stride=columns), :].astype(BF16)
    quarter = rows // 4
    lane = lax.broadcasted_iota(jnp.int32, (quarter, 128), 1)
    packed = jnp.zeros((quarter, 128), F32)
    for k in range(4):
        part = pltpu.roll(acc[k * quarter : (k + 1) * quarter, :], (k * 32 + 128 - 32) % 128, 1)
        packed = jnp.where(lane // 32 == k, part, packed)
    ca_send[...] = packed.astype(BF16)

    pl.semaphore_wait(barrier, expect)

    bufs = {1: (rs_send, rs_got), -1: (ls_send, ls_got), 0: (ca_send, ca_got)}

    def link_copy(i, sign):
        ds, dt = links[i]
        ok, si, ti = there(ds, dt, sign)
        src, dst = bufs[ds]
        if ds != 0:
            dst = dst.at[dt]
        return ok, pltpu.make_async_remote_copy(
            src_ref=src, dst_ref=dst, send_sem=s1_sem.at[i], recv_sem=r1_sem.at[i],
            device_id=dev(c, si, ti), device_id_type=MESH,
        )

    for i in (2, 3, 4, 0, 1):
        ok, copy = link_copy(i, 1)

        @pl.when(ok)
        def _():
            copy.start()

    for i in (0, 1, 3, 4, 2):
        ds, dt = links[i]
        ok, copy = link_copy(i, -1)

        @pl.when(ok)
        def _():
            copy.wait_recv()
            if ds == 0:
                got = ca_got[...].astype(F32)
                for k in range(4):
                    acc[k * quarter : (k + 1) * quarter, :] += pltpu.roll(got, (128 - 32 * k) % 128, 1)
            else:
                got = bufs[ds][1][dt].astype(F32)
                turn = (128 - 32 * dt - (64 if ds < 0 else 0)) % 128
                if turn:
                    got = pltpu.roll(got, turn, 1)
                at = pl.ds(0 if ds > 0 else columns - 1, half, stride=columns)
                acc[at, :] = acc[at, :] + got

    total = acc[...] + bias
    by_row = total.reshape(pairs, 2, columns, 128)
    even = by_row[:, 0].reshape(pairs * columns, 128)
    odd = by_row[:, 1].reshape(pairs * columns, 128)
    lane = lax.broadcasted_iota(jnp.int32, (pairs * columns, 128), 1)
    mixed = jnp.where(
        lane < 16, even,
        jnp.where(
            lane < 32, pltpu.roll(odd, 16, 1),
            jnp.where(lane < 48, pltpu.roll(even, 16, 1), pltpu.roll(odd, 32, 1)),
        ),
    )
    pk[...] = mixed
    tokens = pairs * columns // 2
    left_half = pk[pl.ds(0, tokens, stride=2), :]
    right_half = pk[pl.ds(1, tokens, stride=2), :]
    lane = lax.broadcasted_iota(jnp.int32, (tokens, 128), 1)
    for f in range(frames):
        one = left_half if f == 0 else pltpu.roll(left_half, 128 - 32 * f, 1)
        two = pltpu.roll(right_half, (32 - 32 * f) % 128, 1) if f != 1 else right_half
        both = jnp.where(lane < 32, one, two)
        for m in range(chunks):
            patch[f * chunks + m] = both[m * chunk_tokens : (m + 1) * chunk_tokens, :64].astype(BF16)

    def patch_copy(f, m, ci):
        shard = ((t * frames + f) * (height // 2) + c * pairs) // shard_rows + m
        si, ti = shard // n_t, shard % n_t
        mine = (si == s) & (ti == t) & (c == ci)
        piece = f * chunks + m
        local = pltpu.make_async_copy(patch.at[piece], out_ref.at[s], r2_sem.at[s])
        away = pltpu.make_async_remote_copy(
            src_ref=patch.at[piece], dst_ref=out_ref.at[s],
            send_sem=s2_sem.at[piece * n_c + ci], recv_sem=r2_sem.at[s],
            device_id=dev(ci, si, ti), device_id_type=MESH,
        )
        return mine, local, away

    every = [(f, m, ci) for f in range(frames) for m in range(chunks) for ci in range(n_c)]
    for item in every:
        mine, local, away = patch_copy(*item)

        @pl.when(mine)
        def _():
            local.start()

        @pl.when(jnp.logical_not(mine))
        def _():
            away.start()

    for si in range(n_s):
        pltpu.make_async_copy(patch.at[0], out_ref.at[si], r2_sem.at[si]).wait()
    for i in range(5):
        ok, copy = link_copy(i, 1)

        @pl.when(ok)
        def _():
            copy.wait_send()

    for item in every:
        mine, _, away = patch_copy(*item)

        @pl.when(jnp.logical_not(mine))
        def _():
            away.wait_send()


def tail_kernel(noisy, mask, lat, pw, cw, pb, cb, shift, scale, out, comb, both, inv_ref, mean_ref, sems):
    split = lat.shape[-1]
    width = comb.shape[1]
    step = 512
    z = split // 4

    @pl.when(pl.program_id(0) == 0)
    def _():
        upper = pltpu.make_async_copy(pw, both.at[:split], sems.at[0])
        lower = pltpu.make_async_copy(cw, both.at[split:], sems.at[1])
        upper.start()
        lower.start()
        upper.wait()
        lower.wait()

    parts = comb.shape[0] // out.shape[0]

    @pl.when(pl.program_id(0) % parts == 0)
    def _():
        perm = ones_where(
            (split, split), lambda i, j: j == (i % z) * 4 + (i // z % 2) * 2 + i // (2 * z)
        ).astype(BF16)
        if len(lat.shape) == 3:
            strips, per, _ = lat.shape
            tokens = lat[...].reshape(strips * per, split)
            n, cols = strips * per, 4
            order = ones_where(
                (n, n),
                lambda i, j: j == (i // cols % strips) * per + i // (cols * strips) * cols + i % cols,
            ).astype(BF16)
            tokens = jnp.dot(order, tokens, preferred_element_type=F32).astype(BF16)
        else:
            tokens = lat[...]
        tokens = jnp.dot(tokens, perm, preferred_element_type=F32)
        own = noisy[...].astype(F32).T
        lhs = jnp.concatenate([own, tokens, mask[...].astype(F32)], axis=1).astype(BF16)
        total = None
        for k in range(0, width, step):
            at = slice(k, k + step)
            part = jnp.dot(lhs, both[:, at], preferred_element_type=F32)
            part = part + (pb[:, at] + cb[:, at])
            comb[:, at] = part
            term = jnp.sum(part, axis=-1, keepdims=True)
            total = term if total is None else total + term
        mean = total * (1.0 / width)
        square = None
        for k in range(0, width, step):
            d = comb[:, k : k + step] - mean
            term = jnp.sum(d * d, axis=-1, keepdims=True)
            square = term if square is None else square + term
        mean_ref[...] = jnp.broadcast_to(mean, mean_ref.shape)
        inv_ref[...] = jnp.broadcast_to(lax.rsqrt(square * (1.0 / width) + 1e-06), inv_ref.shape)

    rows = out.shape[0]
    mine = pl.ds(pl.multiple_of(pl.program_id(0) % parts * rows, rows), rows)
    mean, inv = mean_ref[mine, :1], inv_ref[mine, :1]
    for k in range(0, width, step):
        at = slice(k, k + step)
        out[:, at] = ((comb[mine, at] - mean) * inv * (1.0 + scale[:, at]) + shift[:, at]).astype(BF16)


def body(
    section_input, norm_gain, conv_weight, conv_bias, mean_weight, mean_bias, noisy_tokens,
    mask_tokens, patch_weight, patch_bias, context_weight, context_bias, norm_shift, norm_scale,
):
    frames, height, columns, channels = section_input.shape
    n_c, n_s, n_t = lax.axis_size("cfg"), lax.axis_size("seq"), lax.axis_size("tile")
    z = mean_weight.shape[1]
    tokens = noisy_tokens.shape[0]
    shard_rows = tokens // (n_s * columns // 2)
    half = height // n_c
    rows = half * columns
    chunks = half // 2 // shard_rows
    chunk_tokens = shard_rows * (columns // 2)
    vmem = pl.BlockSpec(memory_space=pltpu.VMEM)
    arrived = pl.pallas_call(
        functools.partial(head_kernel, (n_c, n_s, n_t, shard_rows)),
        out_shape=jax.ShapeDtypeStruct((n_s, chunk_tokens, 4 * z), BF16),
        in_specs=[pl.BlockSpec(memory_space=pltpu.HBM)] + [vmem] * 5,
        out_specs=vmem,
        scratch_shapes=[
            pltpu.VMEM((frames * K, 16 * z, channels), BF16),
            pltpu.VMEM((frames, half + 2, columns, channels), BF16),
            pltpu.VMEM((frames, (half + 2) * columns, channels), F32),
            pltpu.VMEM((rows, 128), F32),
            pltpu.VMEM((rows, 128), F32),
            pltpu.VMEM((rows // 2, 128), F32),
            pltpu.VMEM((half, 128), BF16),
            pltpu.VMEM((half, 128), BF16),
            pltpu.VMEM((rows // 4, 128), BF16),
            pltpu.VMEM((2, half, 128), BF16),
            pltpu.VMEM((2, half, 128), BF16),
            pltpu.VMEM((rows // 4, 128), BF16),
            pltpu.VMEM((frames * chunks, chunk_tokens, 4 * z), BF16),
            pltpu.SemaphoreType.DMA,
            pltpu.SemaphoreType.DMA((5,)),
            pltpu.SemaphoreType.DMA((5,)),
            pltpu.SemaphoreType.DMA((frames * chunks * n_c,)),
            pltpu.SemaphoreType.DMA((n_s,)),
        ],
        compiler_params=pltpu.CompilerParams(collective_id=0, has_side_effects=True),
        name="head",
    )(
        section_input, conv_weight.T, norm_gain, mean_weight.T, conv_bias[None], mean_bias[None]
    )
    width = patch_weight.shape[1]
    block = min(tokens, 256)
    per = block // n_s
    if per % 16 == 0 and columns == 8:
        lat = arrived
        lat_spec = pl.BlockSpec((n_s, per, 4 * z), lambda i: (0, i // parts, 0))
    else:
        lat = arrived.reshape(n_s, shard_rows, columns // 2, 4 * z).transpose(1, 0, 2, 3)
        lat = lat.reshape(tokens, 4 * z)
        lat_spec = pl.BlockSpec((block, 4 * z), lambda i: (i // parts, 0))
    parts = 2 if block % 32 == 0 else 1
    tok = lambda n: pl.BlockSpec((block, n), lambda i: (i // parts, 0))
    full = lambda a: pl.BlockSpec(a.shape, lambda i: (0, 0))
    hbm = pl.BlockSpec(memory_space=pl.ANY)
    depth = patch_weight.shape[0] + context_weight.shape[0]
    vecs = [v[None] for v in (patch_bias, context_bias, norm_shift, norm_scale)]
    return pl.pallas_call(
        tail_kernel,
        out_shape=jax.ShapeDtypeStruct((tokens, width), BF16),
        grid=(tokens // block * parts,),
        in_specs=[
            pl.BlockSpec((noisy_tokens.shape[1], block), lambda i: (0, i // parts)),
            tok(mask_tokens.shape[1]), lat_spec, hbm, hbm,
        ]
        + [full(v) for v in vecs],
        out_specs=pl.BlockSpec((block // parts, width), lambda i: (i, 0)),
        scratch_shapes=[
            pltpu.VMEM((block, width), F32),
            pltpu.VMEM((depth, width), BF16),
            pltpu.VMEM((block, 128), F32),
            pltpu.VMEM((block, 128), F32),
            pltpu.SemaphoreType.DMA((2,)),
        ],
        name="tail",
    )(noisy_tokens.T, mask_tokens, lat, patch_weight, context_weight, *vecs)


def solution(mesh):
    placed = (P("tile", None, "seq", None),) + (P(),) * 5
    placed = placed + (P(("seq", "tile"), None),) * 2 + (P(),) * 6
    return jax.shard_map(
        body, mesh=mesh, in_specs=placed, out_specs=P(("seq", "tile"), None), check_vma=False
    )
```
